1024 devices in a mesh: section: 4 (over x_lo, core), ctx: 256 (over y, z, x_hi).
Axes of the slice: x: 4 (x_hi: 2, x_lo: 2; x = x_hi * 2 + x_lo), y: 4, z: 32, core: 2. Of those that a mesh axis runs over, the one named last changes fastest.
Arguments:
- queries: bfloat16 [4, 65536, 1024], P('section', 'ctx'), may hold values from -6 to 6
- keys: bfloat16 [4, 65536, 128], P('section', 'ctx'), may hold values from -6 to 6
- values: bfloat16 [4, 65536, 128], P('section', 'ctx'), may hold values from -6 to 6
- attn_out: bfloat16 [4, 65536, 1024], P('section', 'ctx'), may hold values from -3 to 3
- log_sums: float32 [4, 8, 65536], P('section', None, 'ctx'), may hold values from 2 to 6
- grad_held: bfloat16 [4, 65536, 1024], P('section', 'ctx'), may hold values from -6 to 6
- doc_ids: int32 [65536], P('ctx'), may hold values from 0 to 255, never falling along the last dimension, each value on 1 to 512 neighbouring positions
Outputs:
- grad_queries: bfloat16 [4, 65536, 1024], P('section', 'ctx')
- grad_keys: bfloat16 [4, 65536, 128], P('section', 'ctx')
- grad_values: bfloat16 [4, 65536, 128], P('section', 'ctx')
The draws below stay inside these ranges and needn't reach their ends.
Inputs may be any that keep to these rules, and one draw needn't show every extreme that they name: `doc_ids`: document numbers never fall along the sequence; every document spans at most 512 positions and one spans exactly 512.
All inputs are finite; a program needn't handle non-finite values.
Results may differ from the reference program's by a relative error of at most 0.0049.
Values may be sent and summed in bfloat16 or wider, within the bound.
A program may use at most 32 MiB of HBM per device.

```python
import math
import jax
import jax.numpy as jnp
import numpy as np
from jax import lax

HD = 128
HQ = 8
TOK_DEV = 256
HOPS = 2
DOC_MOST = 512
SEQ = 65536
N_SECTION = 4
N_CTX = 256


def level_of(own_key, shape, cuts, least, high):
    factor_of = 1.0
    for axis_at, blocks in cuts:
        draws = jax.random.uniform(jax.random.fold_in(jax.random.fold_in(own_key, 6), axis_at), (blocks,), jnp.float32, least / len(cuts), high / len(cuts))
        factor_of = factor_of * jnp.repeat(jnp.exp(draws), shape[axis_at] // blocks).reshape((-1,) + (1,) * (len(shape) - 1 - axis_at))
    return factor_of


def split_up(amount, total, most, slope):
    weights = [(1 << 20) // math.isqrt(grade ** slope) + 1 for grade in range(2, amount + 1)]
    surplus, holding = total - most - (amount - 1), [1] * (amount - 1)
    while surplus > 0:
        movable = [i for i in range(amount - 1) if holding[i] < most]
        whole, budget = sum([weights[i] for i in movable]), surplus
        for i in movable:
            extra = min(most - holding[i], max(1, budget * weights[i] // whole), surplus)
            holding[i] = holding[i] + extra
            surplus = surplus - extra
    return np.array([most] + holding)


def uneven_parts(stream_key, number_of, total, reach, slope):
    if number_of == 2:
        one = jax.random.randint(stream_key, (), max(1, total - reach), min(reach, total - 1) + 1)
        return jnp.stack([one, total - one])
    sizes = jnp.asarray(split_up(number_of, total, reach, slope), jnp.int32)
    twos = (number_of - 1) // 2
    source_of, taker = sizes[1:1 + 2 * twos:2], sizes[2:2 + 2 * twos:2]
    room = jnp.minimum(source_of - 1, reach - taker)
    shifted = jax.random.randint(jax.random.fold_in(stream_key, 1), (twos,), 0, 1 << 20) % (room + 1)
    sizes = sizes.at[1:1 + 2 * twos:2].set(source_of - shifted).at[2:2 + 2 * twos:2].set(taker + shifted)
    return sizes[jax.random.permutation(jax.random.fold_in(stream_key, 2), number_of)]


def bell_draw(rng, dims, deviation, bound, pieces=(), kind=jnp.bfloat16):
    level = level_of(rng, dims, pieces, -0.22, 0.18) if pieces else 1.0
    values = jax.random.normal(rng, dims, jnp.float32) * deviation * level
    return jnp.minimum(jnp.maximum(values, -bound), bound).astype(kind)


def setup_inputs(seed: int = 0) -> dict:
    arg_keys = jax.random.split(jax.random.key(seed), 8)
    return {
        "queries": bell_draw(arg_keys[0], (N_SECTION, SEQ, HQ * HD), 1.0, 6.0, ((0, 4), (1, 256))),
        "keys": bell_draw(arg_keys[1], (N_SECTION, SEQ, HD), 1.0, 6.0, ((0, 4), (1, 256))),
        "values": bell_draw(arg_keys[2], (N_SECTION, SEQ, HD), 1.0, 6.0, ((0, 4), (1, 256))),
        "attn_out": bell_draw(arg_keys[3], (N_SECTION, SEQ, HQ * HD), 0.5, 3.0, ((0, 4), (1, 256))),
        "log_sums": jnp.clip(2.0 + 4.0 * jax.random.uniform(arg_keys[4], (N_SECTION, HQ, SEQ), jnp.float32) ** level_of(arg_keys[4], (N_SECTION, HQ, SEQ), ((0, 4), (2, 256)), -0.2, 0.2), 2.0, 6.0),
        "grad_held": bell_draw(arg_keys[5], (N_SECTION, SEQ, HQ * HD), 1.0, 6.0, ((0, 4), (1, 256))),
        "doc_ids": jnp.searchsorted(jnp.cumsum(uneven_parts(arg_keys[6], N_CTX, SEQ, DOC_MOST, 1)), jnp.arange(SEQ), side="right").astype(jnp.int32),
    }


def block_grads(query_block, out_block, grad_block, lse_block, query_docs, query_pos, key_window, value_window, key_docs, key_pos):
    row_count = query_block.shape[0]
    head_count = lse_block.shape[0]
    head_width = key_window.shape[1]
    score_scale = float(head_width) ** -0.5
    q_heads = query_block.astype(jnp.float32).reshape(row_count, head_count, head_width)
    out_heads = out_block.astype(jnp.float32).reshape(row_count, head_count, head_width)
    grad_heads = grad_block.astype(jnp.float32).reshape(row_count, head_count, head_width)
    key_float = key_window.astype(jnp.float32)
    value_float = value_window.astype(jnp.float32)
    deltas = jnp.einsum('qhd,qhd->hq', grad_heads, out_heads)
    scores = jnp.einsum('qhd,kd->hqk', q_heads, key_float) * score_scale
    allowed = (query_docs[:, None] == key_docs[None, :]) & (key_pos[None, :] <= query_pos[:, None]) & (key_pos[None, :] >= 0)
    weights = jnp.where(allowed[None], jnp.exp(scores - lse_block[:, :, None]), jnp.float32(0.0))
    weights_low = weights.astype(jnp.bfloat16).astype(jnp.float32)
    weight_grads = jnp.einsum('qhd,kd->hqk', grad_heads, value_float)
    score_grads = (weights * (weight_grads - deltas[:, :, None])).astype(jnp.bfloat16).astype(jnp.float32)
    grad_q = jnp.einsum('hqk,kd->qhd', score_grads, key_float) * score_scale
    grad_k = jnp.einsum('hqk,qhd->kd', score_grads, q_heads) * score_scale
    grad_v = jnp.einsum('hqk,qhd->kd', weights_low, grad_heads)
    return grad_q.reshape(row_count, head_count * head_width), grad_k, grad_v


def section_grads(queries, keys, values, attn_out, log_sums, arrived, doc_ids):
    sequence = queries.shape[0]
    margin = HOPS * TOK_DEV
    head_width = keys.shape[1]
    window_rows = margin + TOK_DEV
    keys_padded = jnp.concatenate([jnp.zeros((margin, head_width), keys.dtype), keys], axis=0)
    values_padded = jnp.concatenate([jnp.zeros((margin, head_width), values.dtype), values], axis=0)
    docs_padded = jnp.concatenate([jnp.full((margin,), -1, jnp.int32), doc_ids.astype(jnp.int32)], axis=0)
    pos_padded = jnp.arange(sequence + margin, dtype=jnp.int32) - margin

    def advance(accumulated, block_index):
        grad_keys, grad_values = accumulated
        block_start = (block_index * TOK_DEV).astype(jnp.int32)
        query_pos = block_start + jnp.arange(TOK_DEV, dtype=jnp.int32)
        grad_q, grad_k, grad_v = block_grads(
            lax.dynamic_slice_in_dim(queries, block_start, TOK_DEV, 0),
            lax.dynamic_slice_in_dim(attn_out, block_start, TOK_DEV, 0),
            lax.dynamic_slice_in_dim(arrived, block_start, TOK_DEV, 0),
            lax.dynamic_slice_in_dim(log_sums, block_start, TOK_DEV, 1),
            lax.dynamic_slice_in_dim(doc_ids.astype(jnp.int32), block_start, TOK_DEV, 0),
            query_pos,
            lax.dynamic_slice_in_dim(keys_padded, block_start, window_rows, 0),
            lax.dynamic_slice_in_dim(values_padded, block_start, window_rows, 0),
            lax.dynamic_slice_in_dim(docs_padded, block_start, window_rows, 0),
            lax.dynamic_slice_in_dim(pos_padded, block_start, window_rows, 0))
        grad_keys = lax.dynamic_update_slice_in_dim(grad_keys, lax.dynamic_slice_in_dim(grad_keys, block_start, window_rows, 0) + grad_k, block_start, 0)
        grad_values = lax.dynamic_update_slice_in_dim(grad_values, lax.dynamic_slice_in_dim(grad_values, block_start, window_rows, 0) + grad_v, block_start, 0)
        return (grad_keys, grad_values), grad_q.astype(jnp.bfloat16)

    zeros_start = jnp.zeros((sequence + margin, head_width), jnp.float32)
    (grad_keys, grad_values), grad_blocks = lax.scan(advance, (zeros_start, zeros_start), jnp.arange(sequence // TOK_DEV, dtype=jnp.int32))
    grad_queries = grad_blocks.reshape(sequence, queries.shape[1])
    return grad_queries, grad_keys[margin:].astype(jnp.bfloat16), grad_values[margin:].astype(jnp.bfloat16)


def reference(queries, keys, values, attn_out, log_sums, grad_held, doc_ids):
    results = [section_grads(queries[section_index], keys[section_index], values[section_index], attn_out[section_index], log_sums[section_index], grad_held[(section_index + 1) % N_SECTION], doc_ids) for section_index in range(N_SECTION)]
    grad_queries = jnp.stack([entry[0] for entry in results])
    grad_keys = jnp.stack([entry[1] for entry in results])
    grad_values = jnp.stack([entry[2] for entry in results])
    return (grad_queries, grad_keys, grad_values)
```

```python
import functools
import math

import jax
import jax.numpy as jnp
from jax import lax
from jax.experimental import pallas as pl
from jax.experimental.pallas import tpu as pltpu
from jax.sharding import PartitionSpec as P

MESH = pl.DeviceIdType.MESH
LOG2E = math.log2(math.e)
FAR = 1e30
F32 = jnp.float32
BF16 = jnp.bfloat16


def dot_nt(a, b):
    return lax.dot_general(a, b, (((1,), (1,)), ((), ())), preferred_element_type=F32)


def dot_nn(a, b):
    return lax.dot_general(a, b, (((1,), (0,)), ((), ())), preferred_element_type=F32)


def kernel(
    n_section, n_ctx, scale,
    q_hbm, k_hbm, v_hbm, a_hbm, lse_hbm, g_hbm, doc_hbm,
    dq_ref, dk_ref, dv_ref,
    q_s, a_s, g_s, kw, vw, kt, docs, lse_s, bias, p32, p16, ds, del_s, acc_k, acc_v, part, back,
    local_sem, g_send, g_recv, w_send, w_recv, b_send, b_recv,
):
    heads, rows, width = q_s.shape
    half = rows // 2
    sec = lax.axis_index("section")
    ctx = lax.axis_index("ctx")
    sec_up = lax.rem(sec + 1, n_section)
    sec_down = lax.rem(sec + n_section - 1, n_section)
    ahead = [(sec, lax.rem(ctx + d, n_ctx)) for d in (1, 2)]
    behind = [(sec, lax.rem(ctx + n_ctx - d, n_ctx)) for d in (1, 2)]

    barrier = pltpu.get_barrier_semaphore()
    for peer in [(sec_up, ctx), (sec_down, ctx)] + ahead + behind:
        pl.semaphore_signal(barrier, inc=1, device_id=peer, device_id_type=MESH)

    def cols(h):
        return pl.ds(pl.multiple_of(h * width, width), width)

    own = pl.ds(2 * rows, rows)
    fixed = [
        pltpu.make_async_copy(doc_hbm, docs.at[0], local_sem.at[0]),
        pltpu.make_async_copy(lse_hbm, lse_s, local_sem.at[1]),
        pltpu.make_async_copy(k_hbm, kw.at[own], local_sem.at[2]),
        pltpu.make_async_copy(v_hbm, vw.at[own], local_sem.at[3]),
    ]
    for copy in fixed:
        copy.start()

    def q_copy(h):
        return pltpu.make_async_copy(q_hbm.at[:, cols(h)], q_s.at[h], local_sem.at[4 + h])

    def a_copy(h):
        return pltpu.make_async_copy(
            a_hbm.at[:, cols(h)], a_s.at[h], local_sem.at[4 + heads + h]
        )

    def start_local(h, _):
        q_copy(h).start()
        a_copy(h).start()
        return 0

    lax.fori_loop(0, heads, start_local, 0)

    def g_copy(h):
        return pltpu.make_async_remote_copy(
            src_ref=g_hbm.at[:, cols(h)], dst_ref=g_s.at[h],
            send_sem=g_send.at[h], recv_sem=g_recv.at[h],
            device_id=(sec_down, ctx), device_id_type=MESH,
        )

    def window_copy(distance, what):
        src = (k_hbm, doc_hbm, v_hbm)[what]
        place = pl.ds((2 - distance) * rows, rows)
        dst = (kw.at[place], docs.at[distance], vw.at[place])[what]
        at = (distance - 1) * 3 + what
        return pltpu.make_async_remote_copy(
            src_ref=src, dst_ref=dst,
            send_sem=w_send.at[at], recv_sem=w_recv.at[at],
            device_id=ahead[distance - 1], device_id_type=MESH,
        )

    def back_copy(distance):
        return pltpu.make_async_remote_copy(
            src_ref=part.at[distance - 1], dst_ref=back.at[distance - 1],
            send_sem=b_send.at[distance - 1], recv_sem=b_recv.at[distance - 1],
            device_id=behind[distance - 1], device_id_type=MESH,
        )

    pl.semaphore_wait(barrier, 6)
    for what in (0, 1, 2):
        for distance in (1, 2):
            window_copy(distance, what).start()

    def start_g(h, _):
        g_copy(h).start()
        return 0

    lax.fori_loop(0, heads, start_g, 0)

    for copy in fixed:
        copy.wait()
    doc_row = docs[0].astype(F32)
    doc_col = jnp.broadcast_to(doc_row, (half, rows)).T
    doc_col = jnp.concatenate([doc_col, doc_col], axis=1)
    key_at = lax.broadcasted_iota(jnp.int32, (rows, rows), 0)
    query_at = lax.broadcasted_iota(jnp.int32, (rows, rows), 1)
    allowed = (doc_col == jnp.broadcast_to(doc_row, (rows, rows))) & (key_at <= query_at)
    bias[...] = jnp.where(allowed, F32(0.0), F32(-FAR))
    first = docs[0, :, 0:1]
    far_row = jnp.where(docs[0] == first, F32(0.0), F32(FAR))
    c = F32(scale * LOG2E)
    top, bottom = pl.ds(0, half), pl.ds(half, half)
    zeros = jnp.zeros((half, half), BF16)

    def put(h, key_from, count, lanes, weights):
        at = pl.ds(key_from, count)
        p32[h, at, lanes] = weights
        p16[h, at, lanes] = weights.astype(BF16)

    def own_weights(h, _):
        q_copy(h).wait()
        lse = lse_s[pl.ds(h, 1), :] * F32(LOG2E)
        both = slice(0, rows)
        late = slice(half, rows)
        s = dot_nt(kw[pl.ds(2 * rows, half), :], q_s[h])
        put(h, 2 * rows, half, both, jnp.exp2(s * c - lse + bias[0:half, :]))
        s = dot_nt(kw[pl.ds(2 * rows + half, half), :], q_s[h, half:rows, :])
        put(h, 2 * rows + half, half, late, jnp.exp2(s * c - lse[:, half:] + bias[half:, half:]))
        p16[h, 2 * rows + half :, 0:half] = zeros
        ds[h, 2 * rows + half :, 0:half] = zeros
        p16[h, 0:half, half:rows] = zeros
        ds[h, 0:half, half:rows] = zeros
        return 0

    lax.fori_loop(0, heads, own_weights, 0)

    inside = [None, None, None]
    for distance in (2, 1):
        for what in (0, 1):
            window_copy(distance, what).wait_recv()
        place = pl.ds((2 - distance) * rows, rows)
        count = jnp.sum(
            jnp.where(docs[distance] == first, F32(1.0), F32(0.0)), axis=1, keepdims=True
        )
        at = lax.broadcasted_iota(jnp.int32, (rows, width), 0).astype(F32)
        inside[distance] = at >= jnp.broadcast_to(F32(rows) - count, (rows, width))
        kw[place, :] = jnp.where(inside[distance], kw[place, :].astype(F32), 0.0).astype(BF16)

        def far_weights(h, _, distance=distance):
            lse = lse_s[pl.ds(h, 1), :] * F32(LOG2E) + far_row
            start = (2 - distance) * rows
            if distance == 2:
                s = dot_nt(kw[start : start + half, :], q_s[h, 0:half, :])
                put(h, start, half, slice(0, half), jnp.exp2(s * c - lse[:, 0:half]))
                start, many = start + half, half
            else:
                many = rows
            s = dot_nt(kw[start : start + many, :], q_s[h])
            put(h, start, many, slice(0, rows), jnp.exp2(s * c - lse))
            return 0

        lax.fori_loop(0, heads, far_weights, 0)
    kt[...] = kw[...].astype(F32).T.astype(BF16)
    for distance in (2, 1):
        window_copy(distance, 2).wait_recv()
        place = pl.ds((2 - distance) * rows, rows)
        vw[place, :] = jnp.where(inside[distance], vw[place, :].astype(F32), 0.0).astype(BF16)
    acc_k[...] = jnp.zeros_like(acc_k)
    acc_v[...] = jnp.zeros_like(acc_v)
    ones = jnp.ones((8, width), BF16)

    def grads_of(h, key_from, count, lanes, delta):
        at = pl.ds(key_from, count)
        dp = dot_nt(vw[at, :], g_s[h, lanes, :])
        ds[h, at, lanes] = (p32[h, at, lanes] * (dp - delta[:, lanes])).astype(BF16)

    def far_grads(h, _):
        a_copy(h).wait()
        g_copy(h).wait_recv()
        product = g_s[h].astype(F32) * a_s[h].astype(F32)
        high = product.astype(BF16)
        low = (product - high.astype(F32)).astype(BF16)
        delta = dot_nt(ones, high) + dot_nt(ones, low)
        del_s[h] = delta
        delta = delta[0:1, :]
        grads_of(h, 0, half, slice(0, half), delta)
        grads_of(h, half, 2 * rows - half, slice(0, rows), delta)
        acc_v[0 : 2 * rows, :] += dot_nn(p16[h, 0 : 2 * rows, :], g_s[h])
        acc_k[0 : 2 * rows, :] += dot_nn(ds[h, 0 : 2 * rows, :], q_s[h])
        return 0

    lax.fori_loop(0, heads, far_grads, 0)
    for distance in (1, 2):
        place = pl.ds((2 - distance) * rows, rows)
        part[distance - 1, 0] = jnp.where(inside[distance], acc_k[place, :] * F32(scale), 0.0).astype(BF16)
        part[distance - 1, 1] = jnp.where(inside[distance], acc_v[place, :], 0.0).astype(BF16)
        back_copy(distance).start()

    def own_grads(h, _):
        delta = del_s[h, 0:1, :]
        grads_of(h, 2 * rows, half, slice(0, rows), delta)
        grads_of(h, 2 * rows + half, half, slice(half, rows), delta)
        acc_v[own, :] += dot_nn(p16[h, own, :], g_s[h])
        acc_k[own, :] += dot_nn(ds[h, own, :], q_s[h])
        dq = dot_nn(kt[...], ds[h])
        dq_ref[:, cols(h)] = (dq.T * F32(scale)).astype(BF16)
        return 0

    lax.fori_loop(0, heads, own_grads, 0)
    for distance in (1, 2):
        back_copy(distance).wait_recv()
    dk = acc_k[own, :] * F32(scale)
    dv = acc_v[own, :]
    for distance in (1, 2):
        dk = dk + back[distance - 1, 0].astype(F32)
        dv = dv + back[distance - 1, 1].astype(F32)
    dk_ref[...] = dk.astype(BF16)
    dv_ref[...] = dv.astype(BF16)

    def end_g(h, _):
        g_copy(h).wait_send()
        return 0

    lax.fori_loop(0, heads, end_g, 0)
    for distance in (1, 2):
        for what in (0, 1, 2):
            window_copy(distance, what).wait_send()
        back_copy(distance).wait_send()


def per_device(n_section, n_ctx, queries, keys, values, attn_out, log_sums, grad_held, doc_ids):
    rows, width = keys.shape[1:]
    heads = log_sums.shape[1]
    window = 3 * rows
    any_spec = pl.BlockSpec(memory_space=pl.ANY)
    vmem_spec = pl.BlockSpec(memory_space=pltpu.VMEM)
    dq, dk, dv = pl.pallas_call(
        functools.partial(kernel, n_section, n_ctx, float(width) ** -0.5),
        out_shape=(
            jax.ShapeDtypeStruct((rows, heads * width), BF16),
            jax.ShapeDtypeStruct((rows, width), BF16),
            jax.ShapeDtypeStruct((rows, width), BF16),
        ),
        in_specs=[any_spec] * 7,
        out_specs=(vmem_spec,) * 3,
        scratch_shapes=[
            pltpu.VMEM((heads, rows, width), BF16),
            pltpu.VMEM((heads, rows, width), BF16),
            pltpu.VMEM((heads, rows, width), BF16),
            pltpu.VMEM((window, width), BF16),
            pltpu.VMEM((window, width), BF16),
            pltpu.VMEM((width, window), BF16),
            pltpu.VMEM((3, 1, rows), jnp.int32),
            pltpu.VMEM((heads, rows), F32),
            pltpu.VMEM((rows, rows), F32),
            pltpu.VMEM((heads, window, rows), F32),
            pltpu.VMEM((heads, window, rows), BF16),
            pltpu.VMEM((heads, window, rows), BF16),
            pltpu.VMEM((heads, 8, rows), F32),
            pltpu.VMEM((window, width), F32),
            pltpu.VMEM((window, width), F32),
            pltpu.VMEM((2, 2, rows, width), BF16),
            pltpu.VMEM((2, 2, rows, width), BF16),
            pltpu.SemaphoreType.DMA((4 + 2 * heads,)),
            pltpu.SemaphoreType.DMA((heads,)),
            pltpu.SemaphoreType.DMA((heads,)),
            pltpu.SemaphoreType.DMA((6,)),
            pltpu.SemaphoreType.DMA((6,)),
            pltpu.SemaphoreType.DMA((2,)),
            pltpu.SemaphoreType.DMA((2,)),
        ],
        compiler_params=pltpu.CompilerParams(
            collective_id=0, has_side_effects=True, vmem_limit_bytes=32 << 20
        ),
    )(queries[0], keys[0], values[0], attn_out[0], log_sums[0], grad_held[0], doc_ids[None])
    return dq[None], dk[None], dv[None]


def solution(mesh):
    placed = (
        P("section", "ctx", None),
        P("section", "ctx", None),
        P("section", "ctx", None),
        P("section", "ctx", None),
        P("section", None, "ctx"),
        P("section", "ctx", None),
        P("ctx"),
    )
    return jax.shard_map(
        functools.partial(per_device, mesh.shape["section"], mesh.shape["ctx"]),
        mesh=mesh,
        in_specs=placed,
        out_specs=(P("section", "ctx", None),) * 3,
        check_vma=False,
    )
```

```python
import functools
import math

import jax
import jax.numpy as jnp
from jax import lax
from jax.experimental import pallas as pl
from jax.experimental.pallas import tpu as pltpu
from jax.sharding import PartitionSpec as P

MESH = pl.DeviceIdType.MESH
LOG2E = math.log2(math.e)
FAR = 1e30
WIDE = 4
F32 = jnp.float32
BF16 = jnp.bfloat16


def dot_nt(a, b):
    return lax.dot_general(a, b, (((1,), (1,)), ((), ())), preferred_element_type=F32)


def dot_nn(a, b):
    return lax.dot_general(a, b, (((1,), (0,)), ((), ())), preferred_element_type=F32)


def kernel(
    n_section, n_ctx, scale, wide,
    q_hbm, k_hbm, v_hbm, a_hbm, lse_hbm, g_hbm, doc_hbm,
    dq_ref, dk_ref, dv_ref,
    q_s, a_s, g_s, kw, vw, docs, lse_s, lse_row, far_row, del_row, bias, p32, dq_t,
    acc_k, acc_v, part, back,
    local_sem, g_send, g_recv, w_send, w_recv, b_send, b_recv,
):
    heads, rows, width = q_s.shape
    half = rows // 2
    sec = lax.axis_index("section")
    ctx = lax.axis_index("ctx")
    sec_up = lax.rem(sec + 1, n_section)
    sec_down = lax.rem(sec + n_section - 1, n_section)
    ahead = [(sec, lax.rem(ctx + d, n_ctx)) for d in (1, 2)]
    behind = [(sec, lax.rem(ctx + n_ctx - d, n_ctx)) for d in (1, 2)]

    barrier = pltpu.get_barrier_semaphore()
    pl.semaphore_signal(barrier, inc=1, device_id=(sec_up, ctx), device_id_type=MESH)
    for distance in (1, 2):

        @pl.when(ctx >= distance)
        def _(distance=distance):
            pl.semaphore_signal(
                barrier, inc=1, device_id=behind[distance - 1], device_id_type=MESH
            )

    def cols(h):
        return pl.ds(pl.multiple_of(h * width, width), width)

    def lanes(h, many):
        return pl.ds(pl.multiple_of(h * rows, rows), many * rows)

    fixed = [
        pltpu.make_async_copy(doc_hbm, docs.at[0], local_sem.at[0]),
        pltpu.make_async_copy(lse_hbm, lse_s, local_sem.at[1]),
        pltpu.make_async_copy(k_hbm, kw.at[0], local_sem.at[2]),
        pltpu.make_async_copy(v_hbm, vw.at[0], local_sem.at[3]),
    ]
    for copy in fixed:
        copy.start()

    def q_copy(h):
        return pltpu.make_async_copy(q_hbm.at[:, cols(h)], q_s.at[h], local_sem.at[4 + h])

    def a_copy(h):
        return pltpu.make_async_copy(
            a_hbm.at[:, cols(h)], a_s.at[h], local_sem.at[4 + heads + h]
        )

    def g_copy(h):
        return pltpu.make_async_remote_copy(
            src_ref=g_hbm.at[:, cols(h)], dst_ref=g_s.at[h],
            send_sem=g_send.at[h], recv_sem=g_recv.at[h],
            device_id=(sec_down, ctx), device_id_type=MESH,
        )

    def window_copy(distance, what):
        src = (k_hbm, doc_hbm, v_hbm)[what]
        dst = (kw, docs, vw)[what].at[distance]
        at = (distance - 1) * 3 + what
        return pltpu.make_async_remote_copy(
            src_ref=src, dst_ref=dst,
            send_sem=w_send.at[at], recv_sem=w_recv.at[at],
            device_id=ahead[distance - 1], device_id_type=MESH,
        )

    def back_copy(distance):
        return pltpu.make_async_remote_copy(
            src_ref=part.at[distance - 1], dst_ref=back.at[distance - 1],
            send_sem=b_send.at[distance - 1], recv_sem=b_recv.at[distance - 1],
            device_id=behind[distance - 1], device_id_type=MESH,
        )

    reach = jnp.minimum(n_ctx - 1 - ctx, 2)
    pl.semaphore_wait(barrier, 1 + reach)
    for distance in (1, 2):

        @pl.when(reach >= distance)
        def _(distance=distance):
            for what in (0, 1, 2):
                window_copy(distance, what).start()

        @pl.when(ctx < distance)
        def _(distance=distance):
            kw[distance] = jnp.zeros_like(kw[distance])
            vw[distance] = jnp.zeros_like(vw[distance])
            docs[distance] = jnp.full_like(docs[distance], -1)

    def start_copies(h, _):
        g_copy(h).start()
        q_copy(h).start()
        a_copy(h).start()
        return 0

    lax.fori_loop(0, heads, start_copies, 0)

    for copy in fixed:
        copy.wait()
    doc_row = docs[0].astype(F32)
    doc_col = jnp.broadcast_to(doc_row, (half, rows)).T
    doc_col = jnp.concatenate([doc_col, doc_col], axis=1)
    key_at = lax.broadcasted_iota(jnp.int32, (rows, rows), 0)
    query_at = lax.broadcasted_iota(jnp.int32, (rows, rows), 1)
    allowed = (doc_col == jnp.broadcast_to(doc_row, (rows, rows))) & (key_at <= query_at)
    bias[...] = jnp.where(allowed, F32(0.0), F32(-FAR))
    first = docs[0, :, 0:1]
    outside = jnp.where(docs[0] == first, F32(0.0), F32(FAR))
    c = F32(scale * LOG2E)
    for h in range(heads):
        row = lse_s[h : h + 1, :] * F32(LOG2E)
        lse_row[:, h * rows : (h + 1) * rows] = row
        far_row[:, h * rows : (h + 1) * rows] = row + outside

    def own_weights(h, _):
        q_copy(h).wait()
        lse = lse_row[:, lanes(h, 1)]
        s = dot_nt(kw[0, 0:half, :], q_s[h])
        p32[h, 0:half, :] = jnp.exp2(s * c - lse + bias[0:half, :])
        s = dot_nt(kw[0, half:rows, :], q_s[h, half:rows, :])
        p32[h, half:rows, half:rows] = jnp.exp2(s * c - lse[:, half:] + bias[half:, half:])
        return 0

    lax.fori_loop(0, heads, own_weights, 0)

    def turned(block):
        return block.astype(F32).T.astype(BF16)

    acc_k[...] = jnp.zeros_like(acc_k)
    acc_v[...] = jnp.zeros_like(acc_v)
    own_t = turned(kw[0])
    ones = jnp.ones((8, width), BF16)
    zeros = jnp.zeros((half, half), BF16)

    def own_grads(h, _):
        a_copy(h).wait()
        g_copy(h).wait_recv()
        g = g_s[h]
        product = g.astype(F32) * a_s[h].astype(F32)
        high = product.astype(BF16)
        low = (product - high.astype(F32)).astype(BF16)
        delta = (dot_nt(ones, high) + dot_nt(ones, low))[0:1, :]
        del_row[:, lanes(h, 1)] = delta
        p_top = p32[h, 0:half, :]
        p_low = p32[h, half:rows, half:rows]
        ds_top = (p_top * (dot_nt(vw[0, 0:half, :], g) - delta)).astype(BF16)
        ds_low = (
            p_low * (dot_nt(vw[0, half:rows, :], g[half:rows, :]) - delta[:, half:])
        ).astype(BF16)
        p = jnp.concatenate(
            [p_top.astype(BF16), jnp.concatenate([zeros, p_low.astype(BF16)], axis=1)], axis=0
        )
        ds = jnp.concatenate([ds_top, jnp.concatenate([zeros, ds_low], axis=1)], axis=0)
        acc_v[0] += dot_nn(p, g)
        acc_k[0] += dot_nn(ds, q_s[h])
        dq_t[:, lanes(h, 1)] = dot_nn(own_t, ds)
        return 0

    lax.fori_loop(0, heads, own_grads, 0)

    for distance in (2, 1):
        @pl.when(ctx >= distance)
        def _(distance=distance):
            for what in (0, 1, 2):
                window_copy(distance, what).wait_recv()

        count = jnp.sum(
            jnp.where(docs[distance] == first, F32(1.0), F32(0.0)), axis=1, keepdims=True
        )
        at = lax.broadcasted_iota(jnp.int32, (rows, width), 0).astype(F32)
        inside = at >= jnp.broadcast_to(F32(rows) - count, (rows, width))
        k_in = jnp.where(inside, kw[distance].astype(F32), 0.0)
        kw[distance] = k_in.astype(BF16)
        far_t = k_in.T.astype(BF16)
        vw[distance] = jnp.where(inside, vw[distance].astype(F32), 0.0).astype(BF16)

        def far_grads(i, _, distance=distance, far_t=far_t):
            h = i * wide
            at = lanes(h, wide)
            q = q_s[pl.ds(h, wide)].reshape(wide * rows, width)
            g = g_s[pl.ds(h, wide)].reshape(wide * rows, width)
            p = jnp.exp2(dot_nt(kw[distance], q) * c - far_row[:, at])
            dp = dot_nt(vw[distance], g)
            ds = (p * (dp - del_row[:, at])).astype(BF16)
            acc_v[distance] += dot_nn(p.astype(BF16), g)
            acc_k[distance] += dot_nn(ds, q)
            dq = dq_t[:, at] + dot_nn(far_t, ds)
            if distance == 2:
                dq_t[:, at] = dq
            else:
                for j in range(wide):
                    dq_ref[:, cols(h + j)] = (
                        dq[:, j * rows : (j + 1) * rows].T * F32(scale)
                    ).astype(BF16)
            return 0

        lax.fori_loop(0, heads // wide, far_grads, 0)
        part[distance - 1, 0] = jnp.where(inside, acc_k[distance] * F32(scale), 0.0).astype(BF16)
        part[distance - 1, 1] = jnp.where(inside, acc_v[distance], 0.0).astype(BF16)

        @pl.when(ctx >= distance)
        def _(distance=distance):
            back_copy(distance).start()

    for distance in (2, 1):

        @pl.when(reach >= distance)
        def _(distance=distance):
            back_copy(distance).wait_recv()

        @pl.when(reach < distance)
        def _(distance=distance):
            back[distance - 1] = jnp.zeros_like(back[distance - 1])

    dk = acc_k[0] * F32(scale)
    dv = acc_v[0]
    for distance in (1, 2):
        dk = dk + back[distance - 1, 0].astype(F32)
        dv = dv + back[distance - 1, 1].astype(F32)
    dk_ref[...] = dk.astype(BF16)
    dv_ref[...] = dv.astype(BF16)

    def end_g(h, _):
        g_copy(h).wait_send()
        return 0

    lax.fori_loop(0, heads, end_g, 0)
    for distance in (1, 2):

        @pl.when(reach >= distance)
        def _(distance=distance):
            for what in (0, 1, 2):
                window_copy(distance, what).wait_send()

        @pl.when(ctx >= distance)
        def _(distance=distance):
            back_copy(distance).wait_send()


def put_out(dq_ref, dk_ref, dv_ref, dq_out, dk_out, dv_out, sem):
    copies = [
        pltpu.make_async_copy(dq_ref, dq_out.at[0], sem.at[0]),
        pltpu.make_async_copy(dk_ref, dk_out.at[0], sem.at[1]),
        pltpu.make_async_copy(dv_ref, dv_out.at[0], sem.at[2]),
    ]
    for copy in copies:
        copy.start()
    for copy in copies:
        copy.wait()


def per_device(n_section, n_ctx, queries, keys, values, attn_out, log_sums, grad_held, doc_ids):
    rows, width = keys.shape[1:]
    heads = log_sums.shape[1]
    hbm_spec = pl.BlockSpec(memory_space=pltpu.HBM)
    vmem_spec = pl.BlockSpec(memory_space=pltpu.VMEM)
    dq, dk, dv = pl.pallas_call(
        functools.partial(kernel, n_section, n_ctx, float(width) ** -0.5, WIDE),
        out_shape=(
            jax.ShapeDtypeStruct((rows, heads * width), BF16),
            jax.ShapeDtypeStruct((rows, width), BF16),
            jax.ShapeDtypeStruct((rows, width), BF16),
        ),
        in_specs=[hbm_spec] * 7,
        out_specs=(vmem_spec,) * 3,
        scratch_shapes=[
            pltpu.VMEM((heads, rows, width), BF16),
            pltpu.VMEM((heads, rows, width), BF16),
            pltpu.VMEM((heads, rows, width), BF16),
            pltpu.VMEM((3, rows, width), BF16),
            pltpu.VMEM((3, rows, width), BF16),
            pltpu.VMEM((3, 1, rows), jnp.int32),
            pltpu.VMEM((heads, rows), F32),
            pltpu.VMEM((1, heads * rows), F32),
            pltpu.VMEM((1, heads * rows), F32),
            pltpu.VMEM((1, heads * rows), F32),
            pltpu.VMEM((rows, rows), F32),
            pltpu.VMEM((heads, rows, rows), F32),
            pltpu.VMEM((width, heads * rows), F32),
            pltpu.VMEM((3, rows, width), F32),
            pltpu.VMEM((3, rows, width), F32),
            pltpu.VMEM((2, 2, rows, width), BF16),
            pltpu.VMEM((2, 2, rows, width), BF16),
            pltpu.SemaphoreType.DMA((4 + 2 * heads,)),
            pltpu.SemaphoreType.DMA((heads,)),
            pltpu.SemaphoreType.DMA((heads,)),
            pltpu.SemaphoreType.DMA((6,)),
            pltpu.SemaphoreType.DMA((6,)),
            pltpu.SemaphoreType.DMA((2,)),
            pltpu.SemaphoreType.DMA((2,)),
        ],
        compiler_params=pltpu.CompilerParams(
            collective_id=0, has_side_effects=True, vmem_limit_bytes=32 << 20
        ),
    )(
        *(
            pltpu.with_memory_space_constraint(operand, pltpu.HBM)
            for operand in (
                queries[0], keys[0], values[0], attn_out[0], log_sums[0], grad_held[0], doc_ids[None]
            )
        )
    )
    return pl.pallas_call(
        put_out,
        out_shape=tuple(jax.ShapeDtypeStruct((1,) + x.shape, x.dtype) for x in (dq, dk, dv)),
        in_specs=[vmem_spec] * 3,
        out_specs=(hbm_spec,) * 3,
        scratch_shapes=[pltpu.SemaphoreType.DMA((3,))],
        compiler_params=pltpu.CompilerParams(vmem_limit_bytes=4 << 20),
    )(dq, dk, dv)


def solution(mesh):
    placed = (
        P("section", "ctx", None),
        P("section", "ctx", None),
        P("section", "ctx", None),
        P("section", "ctx", None),
        P("section", None, "ctx"),
        P("section", "ctx", None),
        P("ctx"),
    )
    return jax.shard_map(
        functools.partial(per_device, mesh.shape["section"], mesh.shape["ctx"]),
        mesh=mesh,
        in_specs=placed,
        out_specs=(P("section", "ctx", None),) * 3,
        check_vma=False,
    )
```

```python
import functools
import math

import jax
import jax.numpy as jnp
from jax import lax
from jax.experimental import pallas as pl
from jax.experimental.pallas import tpu as pltpu
from jax.sharding import PartitionSpec as P

MESH = pl.DeviceIdType.MESH
LOG2E = math.log2(math.e)
FAR = 1e30
WIDE = 4
F32 = jnp.float32
BF16 = jnp.bfloat16


def dot_nt(a, b):
    return lax.dot_general(a, b, (((1,), (1,)), ((), ())), preferred_element_type=F32)


def dot_nn(a, b):
    return lax.dot_general(a, b, (((1,), (0,)), ((), ())), preferred_element_type=F32)


def kernel(
    n_section, n_ctx, scale, wide,
    q_hbm, k_hbm, v_hbm, a_hbm, lse_hbm, g_hbm, doc_hbm,
    dq_ref, dk_ref, dv_ref,
    q_s, a_s, g_s, kw, vw, docs, lse_s, lse_row, far_row, del_row, bias, p32, dq_t,
    p_far, ds_far, far_t, acc_k, acc_v, part, back,
    local_sem, g_send, g_recv, w_send, w_recv, b_send, b_recv,
):
    heads, rows, width = q_s.shape
    half = rows // 2
    sec = lax.axis_index("section")
    ctx = lax.axis_index("ctx")
    sec_up = lax.rem(sec + 1, n_section)
    sec_down = lax.rem(sec + n_section - 1, n_section)
    sooner = 2 - lax.rem(ctx, 2)
    later = 3 - sooner

    barrier = pltpu.get_barrier_semaphore()
    pl.semaphore_signal(barrier, inc=1, device_id=(sec_up, ctx), device_id_type=MESH)
    for distance in (1, 2):

        @pl.when(ctx >= distance)
        def _(distance=distance):
            pl.semaphore_signal(
                barrier, inc=1, device_id=(sec, ctx - distance), device_id_type=MESH
            )

    def cols(h):
        return pl.ds(pl.multiple_of(h * width, width), width)

    def lanes(h, many):
        return pl.ds(pl.multiple_of(h * rows, rows), many * rows)

    fixed = [
        pltpu.make_async_copy(doc_hbm, docs.at[0], local_sem.at[0]),
        pltpu.make_async_copy(lse_hbm, lse_s, local_sem.at[1]),
        pltpu.make_async_copy(k_hbm, kw.at[0], local_sem.at[2]),
        pltpu.make_async_copy(v_hbm, vw.at[0], local_sem.at[3]),
    ]
    for copy in fixed:
        copy.start()

    def q_copy(h):
        return pltpu.make_async_copy(q_hbm.at[:, cols(h)], q_s.at[h], local_sem.at[4 + h])

    def a_copy(h):
        return pltpu.make_async_copy(
            a_hbm.at[:, cols(h)], a_s.at[h], local_sem.at[4 + heads + h]
        )

    def g_copy(h):
        return pltpu.make_async_remote_copy(
            src_ref=g_hbm.at[:, cols(h)], dst_ref=g_s.at[h],
            send_sem=g_send.at[h], recv_sem=g_recv.at[h],
            device_id=(sec_down, ctx), device_id_type=MESH,
        )

    def window_copy(distance, what):
        src = (k_hbm, doc_hbm, v_hbm)[what]
        dst = (kw, docs, vw)[what].at[distance]
        at = (distance - 1) * 3 + what
        return pltpu.make_async_remote_copy(
            src_ref=src, dst_ref=dst,
            send_sem=w_send.at[at], recv_sem=w_recv.at[at],
            device_id=(sec, lax.rem(ctx + distance, n_ctx)), device_id_type=MESH,
        )

    def back_copy(distance, what):
        at = (distance - 1) * 2 + what
        return pltpu.make_async_remote_copy(
            src_ref=part.at[at], dst_ref=back.at[at],
            send_sem=b_send.at[at], recv_sem=b_recv.at[at],
            device_id=(sec, lax.rem(ctx + n_ctx - distance, n_ctx)), device_id_type=MESH,
        )

    reach = jnp.minimum(n_ctx - 1 - ctx, 2)
    pl.semaphore_wait(barrier, 1 + reach)
    for distance in (sooner, later):

        @pl.when(reach >= distance)
        def _(distance=distance):
            for what in (0, 1, 2):
                window_copy(distance, what).start()

    def start_copies(h, _):
        g_copy(h).start()
        q_copy(h).start()
        a_copy(h).start()
        return 0

    lax.fori_loop(0, heads, start_copies, 0)

    for copy in fixed:
        copy.wait()
    doc_row = docs[0].astype(F32)
    doc_col = jnp.broadcast_to(doc_row, (half, rows)).T
    doc_col = jnp.concatenate([doc_col, doc_col], axis=1)
    key_at = lax.broadcasted_iota(jnp.int32, (rows, rows), 0)
    query_at = lax.broadcasted_iota(jnp.int32, (rows, rows), 1)
    allowed = (doc_col == jnp.broadcast_to(doc_row, (rows, rows))) & (key_at <= query_at)
    bias[...] = jnp.where(allowed, F32(0.0), F32(-FAR))
    first = docs[0, :, 0:1]
    outside = jnp.where(docs[0] == first, F32(0.0), F32(FAR))
    c = F32(scale * LOG2E)
    for h in range(heads):
        row = lse_s[h : h + 1, :] * F32(LOG2E)
        lse_row[:, h * rows : (h + 1) * rows] = row
        far_row[:, h * rows : (h + 1) * rows] = row + outside

    def own_weights(h, _):
        q_copy(h).wait()
        lse = lse_row[:, lanes(h, 1)]
        s = dot_nt(kw[0, 0:half, :], q_s[h])
        p32[h, 0:half, :] = jnp.exp2(s * c - lse + bias[0:half, :])
        s = dot_nt(kw[0, half:rows, :], q_s[h, half:rows, :])
        p32[h, half:rows, half:rows] = jnp.exp2(s * c - lse[:, half:] + bias[half:, half:])
        return 0

    lax.fori_loop(0, heads, own_weights, 0)

    def turned(block):
        return block.astype(F32).T.astype(BF16)

    acc_k[...] = jnp.zeros_like(acc_k)
    acc_v[...] = jnp.zeros_like(acc_v)
    own_t = turned(kw[0])
    ones = jnp.ones((8, width), BF16)
    zeros = jnp.zeros((half, half), BF16)

    def own_grads(h, _):
        a_copy(h).wait()
        g_copy(h).wait_recv()
        g = g_s[h]
        product = g.astype(F32) * a_s[h].astype(F32)
        high = product.astype(BF16)
        low = (product - high.astype(F32)).astype(BF16)
        delta = (dot_nt(ones, high) + dot_nt(ones, low))[0:1, :]
        del_row[:, lanes(h, 1)] = delta
        p_top = p32[h, 0:half, :]
        p_low = p32[h, half:rows, half:rows]
        ds_top = (p_top * (dot_nt(vw[0, 0:half, :], g) - delta)).astype(BF16)
        ds_low = (
            p_low * (dot_nt(vw[0, half:rows, :], g[half:rows, :]) - delta[:, half:])
        ).astype(BF16)
        p = jnp.concatenate(
            [p_top.astype(BF16), jnp.concatenate([zeros, p_low.astype(BF16)], axis=1)], axis=0
        )
        ds = jnp.concatenate([ds_top, jnp.concatenate([zeros, ds_low], axis=1)], axis=0)
        acc_v[0] += dot_nn(p, g)
        acc_k[0] += dot_nn(ds, q_s[h])
        dq_t[:, lanes(h, 1)] = dot_nn(own_t, ds)
        return 0

    lax.fori_loop(0, heads, own_grads, 0)

    def heads_of(ref, i):
        return ref[pl.ds(i * wide, wide)].reshape(wide * rows, width)

    def far_block(distance, place):
        window_copy(distance, 0).wait_recv()
        window_copy(distance, 1).wait_recv()
        count = jnp.sum(
            jnp.where(docs[distance] == first, F32(1.0), F32(0.0)), axis=1, keepdims=True
        )

        def inside():
            at = lax.broadcasted_iota(jnp.int32, (rows, width), 0).astype(F32)
            return at >= jnp.broadcast_to(F32(rows) - count, (rows, width))

        def send(what, total):
            part[(distance - 1) * 2 + what] = jnp.where(inside(), total, 0.0).astype(BF16)
            back_copy(distance, what).start()

        k_in = jnp.where(inside(), kw[distance].astype(F32), 0.0)
        kw[distance] = k_in.astype(BF16)
        far_t[:, place] = k_in.T.astype(BF16)

        def weights(i, _):
            at = lanes(i * wide, wide)
            p = jnp.exp2(dot_nt(kw[distance], heads_of(q_s, i)) * c - far_row[:, at])
            p_far[:, at] = p
            acc_v[distance] += dot_nn(p.astype(BF16), heads_of(g_s, i))
            return 0

        lax.fori_loop(0, heads // wide, weights, 0)
        send(1, acc_v[distance])
        window_copy(distance, 2).wait_recv()
        vw[distance] = jnp.where(inside(), vw[distance].astype(F32), 0.0).astype(BF16)

        def score_grads(i, _):
            at = lanes(i * wide, wide)
            dp = dot_nt(vw[distance], heads_of(g_s, i))
            ds = (p_far[:, at] * (dp - del_row[:, at])).astype(BF16)
            ds_far[place, at] = ds
            acc_k[distance] += dot_nn(ds, heads_of(q_s, i))
            return 0

        lax.fori_loop(0, heads // wide, score_grads, 0)
        send(0, acc_k[distance] * F32(scale))

    for at, distance in enumerate((sooner, later)):
        place = slice(at * rows, (at + 1) * rows)

        @pl.when(ctx >= distance)
        def _(distance=distance, place=place):
            far_block(distance, place)

        @pl.when(ctx < distance)
        def _(place=place):
            far_t[:, place] = jnp.zeros((width, rows), BF16)
            ds_far[place, :] = jnp.zeros((rows, heads * rows), BF16)

    def query_grads(i, _):
        at = lanes(i * wide, wide)
        dq = dq_t[:, at] + dot_nn(far_t[...], ds_far[:, at])
        for j in range(wide):
            dq_ref[:, cols(i * wide + j)] = (
                dq[:, j * rows : (j + 1) * rows].T * F32(scale)
            ).astype(BF16)
        return 0

    lax.fori_loop(0, heads // wide, query_grads, 0)

    dk = acc_k[0] * F32(scale)
    dv = acc_v[0]
    for distance in (1, 2):

        @pl.when(reach >= distance)
        def _(distance=distance):
            for what in (0, 1):
                back_copy(distance, what).wait_recv()

        @pl.when(reach < distance)
        def _(distance=distance):
            for what in (0, 1):
                at = (distance - 1) * 2 + what
                back[at] = jnp.zeros_like(back[at])

        dk = dk + back[distance * 2 - 2].astype(F32)
        dv = dv + back[distance * 2 - 1].astype(F32)
    dk_ref[...] = dk.astype(BF16)
    dv_ref[...] = dv.astype(BF16)

    def end_g(h, _):
        g_copy(h).wait_send()
        return 0

    lax.fori_loop(0, heads, end_g, 0)
    for distance in (1, 2):

        @pl.when(reach >= distance)
        def _(distance=distance):
            for what in (0, 1, 2):
                window_copy(distance, what).wait_send()

        @pl.when(ctx >= distance)
        def _(distance=distance):
            for what in (0, 1):
                back_copy(distance, what).wait_send()


def put_out(dq_ref, dk_ref, dv_ref, dq_out, dk_out, dv_out, sem):
    copies = [
        pltpu.make_async_copy(dq_ref, dq_out.at[0], sem.at[0]),
        pltpu.make_async_copy(dk_ref, dk_out.at[0], sem.at[1]),
        pltpu.make_async_copy(dv_ref, dv_out.at[0], sem.at[2]),
    ]
    for copy in copies:
        copy.start()
    for copy in copies:
        copy.wait()


def per_device(n_section, n_ctx, queries, keys, values, attn_out, log_sums, grad_held, doc_ids):
    rows, width = keys.shape[1:]
    heads = log_sums.shape[1]
    hbm_spec = pl.BlockSpec(memory_space=pltpu.HBM)
    vmem_spec = pl.BlockSpec(memory_space=pltpu.VMEM)
    dq, dk, dv = pl.pallas_call(
        functools.partial(kernel, n_section, n_ctx, float(width) ** -0.5, WIDE),
        out_shape=(
            jax.ShapeDtypeStruct((rows, heads * width), BF16),
            jax.ShapeDtypeStruct((rows, width), BF16),
            jax.ShapeDtypeStruct((rows, width), BF16),
        ),
        in_specs=[hbm_spec] * 7,
        out_specs=(vmem_spec,) * 3,
        scratch_shapes=[
            pltpu.VMEM((heads, rows, width), BF16),
            pltpu.VMEM((heads, rows, width), BF16),
            pltpu.VMEM((heads, rows, width), BF16),
            pltpu.VMEM((3, rows, width), BF16),
            pltpu.VMEM((3, rows, width), BF16),
            pltpu.VMEM((3, 1, rows), jnp.int32),
            pltpu.VMEM((heads, rows), F32),
            pltpu.VMEM((1, heads * rows), F32),
            pltpu.VMEM((1, heads * rows), F32),
            pltpu.VMEM((1, heads * rows), F32),
            pltpu.VMEM((rows, rows), F32),
            pltpu.VMEM((heads, rows, rows), F32),
            pltpu.VMEM((width, heads * rows), F32),
            pltpu.VMEM((rows, heads * rows), F32),
            pltpu.VMEM((2 * rows, heads * rows), BF16),
            pltpu.VMEM((width, 2 * rows), BF16),
            pltpu.VMEM((3, rows, width), F32),
            pltpu.VMEM((3, rows, width), F32),
            pltpu.VMEM((4, rows, width), BF16),
            pltpu.VMEM((4, rows, width), BF16),
            pltpu.SemaphoreType.DMA((4 + 2 * heads,)),
            pltpu.SemaphoreType.DMA((heads,)),
            pltpu.SemaphoreType.DMA((heads,)),
            pltpu.SemaphoreType.DMA((6,)),
            pltpu.SemaphoreType.DMA((6,)),
            pltpu.SemaphoreType.DMA((4,)),
            pltpu.SemaphoreType.DMA((4,)),
        ],
        compiler_params=pltpu.CompilerParams(
            collective_id=0, has_side_effects=True, vmem_limit_bytes=32 << 20
        ),
    )(
        *(
            pltpu.with_memory_space_constraint(operand, pltpu.HBM)
            for operand in (
                queries[0], keys[0], values[0], attn_out[0], log_sums[0], grad_held[0], doc_ids[None]
            )
        )
    )
    return pl.pallas_call(
        put_out,
        out_shape=tuple(jax.ShapeDtypeStruct((1,) + x.shape, x.dtype) for x in (dq, dk, dv)),
        in_specs=[vmem_spec] * 3,
        out_specs=(hbm_spec,) * 3,
        scratch_shapes=[pltpu.SemaphoreType.DMA((3,))],
        compiler_params=pltpu.CompilerParams(vmem_limit_bytes=4 << 20),
    )(dq, dk, dv)


def solution(mesh):
    placed = (
        P("section", "ctx", None),
        P("section", "ctx", None),
        P("section", "ctx", None),
        P("section", "ctx", None),
        P("section", None, "ctx"),
        P("section", "ctx", None),
        P("ctx"),
    )
    return jax.shard_map(
        functools.partial(per_device, mesh.shape["section"], mesh.shape["ctx"]),
        mesh=mesh,
        in_specs=placed,
        out_specs=(P("section", "ctx", None),) * 3,
        check_vma=False,
    )
```

```python
import functools
import math

import jax
import jax.numpy as jnp
from jax import lax
from jax.experimental import pallas as pl
from jax.experimental.pallas import tpu as pltpu
from jax.sharding import PartitionSpec as P

MESH = pl.DeviceIdType.MESH
LOG2E = math.log2(math.e)
FAR = 1e30
WIDE = 4
RUN = 64
F32 = jnp.float32
BF16 = jnp.bfloat16


def dot_nt(a, b):
    return lax.dot_general(a, b, (((1,), (1,)), ((), ())), preferred_element_type=F32)


def dot_nn(a, b):
    return lax.dot_general(a, b, (((1,), (0,)), ((), ())), preferred_element_type=F32)


def kernel(
    n_section, n_ctx, scale, wide,
    q_hbm, k_hbm, v_hbm, a_hbm, lse_hbm, g_hbm, doc_hbm,
    dq_ref, dk_ref, dv_ref,
    q_s, a_s, g_s, kw, vw, docs, lse_s, lse_row, far_row, del_row, bias, p32, dq_t,
    p_far, ds_far, far_t, acc_k, acc_v, part, back,
    local_sem, g_send, g_recv, w_send, w_recv, b_send, b_recv, go_sem,
):
    heads, rows, width = q_s.shape
    half = rows // 2
    sec = lax.axis_index("section")
    ctx = lax.axis_index("ctx")
    sec_up = lax.rem(sec + 1, n_section)
    sec_down = lax.rem(sec + n_section - 1, n_section)
    sooner = 2 - lax.rem(ctx, 2)
    later = 3 - sooner

    barrier = pltpu.get_barrier_semaphore()
    at_end = ((lax.rem(ctx, RUN) >= RUN - 2) & (ctx < n_ctx - 2)).astype(jnp.int32)
    before_end = ((lax.rem(ctx + 2, RUN) >= RUN - 2) & (ctx < n_ctx - 4)).astype(jnp.int32)
    odd = lax.rem(ctx, 2)
    end_odd = at_end * odd
    end_even = at_end - end_odd
    greeted = ctx - 2 * at_end
    pl.semaphore_signal(barrier, inc=1, device_id=(sec_up, greeted), device_id_type=MESH)
    for distance in (1, 2):

        @pl.when((ctx >= distance) & ((distance == 2) | (end_odd == 0)))
        def _(distance=distance):
            pl.semaphore_signal(
                barrier, inc=1, device_id=(sec, ctx - distance), device_id_type=MESH
            )

    def cols(h):
        return pl.ds(pl.multiple_of(h * width, width), width)

    def lanes(h, many):
        return pl.ds(pl.multiple_of(h * rows, rows), many * rows)

    fixed = [
        pltpu.make_async_copy(doc_hbm, docs.at[0], local_sem.at[0]),
        pltpu.make_async_copy(lse_hbm, lse_s, local_sem.at[1]),
        pltpu.make_async_copy(k_hbm, kw.at[0], local_sem.at[2]),
        pltpu.make_async_copy(v_hbm, vw.at[0], local_sem.at[3]),
    ]
    for copy in fixed:
        copy.start()

    def q_copy(h):
        return pltpu.make_async_copy(q_hbm.at[:, cols(h)], q_s.at[h], local_sem.at[4 + h])

    def a_copy(h):
        return pltpu.make_async_copy(
            a_hbm.at[:, cols(h)], a_s.at[h], local_sem.at[4 + heads + h]
        )

    def start_local(h, _):
        q_copy(h).start()
        a_copy(h).start()
        return 0

    lax.fori_loop(0, heads, start_local, 0)

    def g_copy(h):
        return pltpu.make_async_remote_copy(
            src_ref=g_hbm.at[:, cols(h)], dst_ref=g_s.at[h],
            send_sem=g_send.at[h], recv_sem=g_recv.at[h],
            device_id=(sec_down, ctx), device_id_type=MESH,
        )

    def window_copy(distance, what):
        src = (k_hbm, doc_hbm, v_hbm)[what]
        dst = (kw, docs, vw)[what].at[distance]
        at = (distance - 1) * 3 + what
        return pltpu.make_async_remote_copy(
            src_ref=src, dst_ref=dst,
            send_sem=w_send.at[at], recv_sem=w_recv.at[at],
            device_id=(sec, lax.rem(ctx + distance, n_ctx)), device_id_type=MESH,
        )

    def back_copy(distance, what):
        at = (distance - 1) * 2 + what
        return pltpu.make_async_remote_copy(
            src_ref=part.at[at], dst_ref=back.at[at],
            send_sem=b_send.at[at], recv_sem=b_recv.at[at],
            device_id=(sec, lax.rem(ctx + n_ctx - distance, n_ctx)), device_id_type=MESH,
        )

    reach = jnp.minimum(n_ctx - 1 - ctx, 2)
    pl.semaphore_wait(barrier, 1 + reach - at_end - end_even + before_end)

    @pl.when(before_end == 1)
    def _():
        pl.semaphore_signal(
            go_sem, inc=1, device_id=(sec, lax.rem(ctx + 2, n_ctx)), device_id_type=MESH
        )

    @pl.when(before_end * odd == 1)
    def _():
        pl.semaphore_signal(
            go_sem, inc=1, device_id=(sec, lax.rem(ctx + 1, n_ctx)), device_id_type=MESH
        )

    for distance in (sooner, later):

        @pl.when(reach >= distance)
        def _(distance=distance):
            for what in (0, 1, 2):
                window_copy(distance, what).start()

        if distance is sooner:

            @pl.when(end_even == 1)
            def _():
                pl.semaphore_wait(go_sem, 2)

    @pl.when(end_odd == 1)
    def _():
        pl.semaphore_wait(go_sem, 1)

    def start_g(h, _):
        g_copy(h).start()
        return 0

    lax.fori_loop(0, heads, start_g, 0)

    for copy in fixed:
        copy.wait()
    doc_row = docs[0].astype(F32)
    doc_col = jnp.broadcast_to(doc_row, (half, rows)).T
    doc_col = jnp.concatenate([doc_col, doc_col], axis=1)
    key_at = lax.broadcasted_iota(jnp.int32, (rows, rows), 0)
    query_at = lax.broadcasted_iota(jnp.int32, (rows, rows), 1)
    allowed = (doc_col == jnp.broadcast_to(doc_row, (rows, rows))) & (key_at <= query_at)
    bias[...] = jnp.where(allowed, F32(0.0), F32(-FAR))
    first = docs[0, :, 0:1]
    outside = jnp.where(docs[0] == first, F32(0.0), F32(FAR))
    c = F32(scale * LOG2E)
    for h in range(heads):
        row = lse_s[h : h + 1, :] * F32(LOG2E)
        lse_row[:, h * rows : (h + 1) * rows] = row
        far_row[:, h * rows : (h + 1) * rows] = row + outside

    def own_weights(h, _):
        q_copy(h).wait()
        lse = lse_row[:, lanes(h, 1)]
        s = dot_nt(kw[0, 0:half, :], q_s[h])
        p32[h, 0:half, :] = jnp.exp2(s * c - lse + bias[0:half, :])
        s = dot_nt(kw[0, half:rows, :], q_s[h, half:rows, :])
        p32[h, half:rows, half:rows] = jnp.exp2(s * c - lse[:, half:] + bias[half:, half:])
        return 0

    lax.fori_loop(0, heads, own_weights, 0)

    def turned(block):
        return block.astype(F32).T.astype(BF16)

    acc_k[...] = jnp.zeros_like(acc_k)
    acc_v[...] = jnp.zeros_like(acc_v)
    own_t = turned(kw[0])
    ones = jnp.ones((8, width), BF16)
    zeros = jnp.zeros((half, half), BF16)

    def own_grads(h, _):
        a_copy(h).wait()
        g_copy(h).wait_recv()
        g = g_s[h]
        product = g.astype(F32) * a_s[h].astype(F32)
        high = product.astype(BF16)
        low = (product - high.astype(F32)).astype(BF16)
        delta = (dot_nt(ones, high) + dot_nt(ones, low))[0:1, :]
        del_row[:, lanes(h, 1)] = delta
        p_top = p32[h, 0:half, :]
        p_low = p32[h, half:rows, half:rows]
        ds_top = (p_top * (dot_nt(vw[0, 0:half, :], g) - delta)).astype(BF16)
        ds_low = (
            p_low * (dot_nt(vw[0, half:rows, :], g[half:rows, :]) - delta[:, half:])
        ).astype(BF16)
        p = jnp.concatenate(
            [p_top.astype(BF16), jnp.concatenate([zeros, p_low.astype(BF16)], axis=1)], axis=0
        )
        ds = jnp.concatenate([ds_top, jnp.concatenate([zeros, ds_low], axis=1)], axis=0)
        acc_v[0] += dot_nn(p, g)
        acc_k[0] += dot_nn(ds, q_s[h])
        dq_t[:, lanes(h, 1)] = dot_nn(own_t, ds)
        return 0

    lax.fori_loop(0, heads, own_grads, 0)

    def heads_of(ref, i):
        return ref[pl.ds(i * wide, wide)].reshape(wide * rows, width)

    def far_block(distance, place):
        window_copy(distance, 0).wait_recv()
        window_copy(distance, 1).wait_recv()
        count = jnp.sum(
            jnp.where(docs[distance] == first, F32(1.0), F32(0.0)), axis=1, keepdims=True
        )

        def inside():
            at = lax.broadcasted_iota(jnp.int32, (rows, width), 0).astype(F32)
            return at >= jnp.broadcast_to(F32(rows) - count, (rows, width))

        def send(what, total):
            part[(distance - 1) * 2 + what] = jnp.where(inside(), total, 0.0).astype(BF16)
            back_copy(distance, what).start()

        k_in = jnp.where(inside(), kw[distance].astype(F32), 0.0)
        kw[distance] = k_in.astype(BF16)
        far_t[:, place] = k_in.T.astype(BF16)

        def weights(i, _):
            at = lanes(i * wide, wide)
            p = jnp.exp2(dot_nt(kw[distance], heads_of(q_s, i)) * c - far_row[:, at])
            p_far[:, at] = p
            acc_v[distance] += dot_nn(p.astype(BF16), heads_of(g_s, i))
            return 0

        lax.fori_loop(0, heads // wide, weights, 0)
        send(1, acc_v[distance])
        window_copy(distance, 2).wait_recv()
        vw[distance] = jnp.where(inside(), vw[distance].astype(F32), 0.0).astype(BF16)

        def score_grads(i, _):
            at = lanes(i * wide, wide)
            dp = dot_nt(vw[distance], heads_of(g_s, i))
            ds = (p_far[:, at] * (dp - del_row[:, at])).astype(BF16)
            ds_far[place, at] = ds
            acc_k[distance] += dot_nn(ds, heads_of(q_s, i))
            return 0

        lax.fori_loop(0, heads // wide, score_grads, 0)
        send(0, acc_k[distance] * F32(scale))

    for at, distance in enumerate((sooner, later)):
        place = slice(at * rows, (at + 1) * rows)

        @pl.when(ctx >= distance)
        def _(distance=distance, place=place):
            far_block(distance, place)

        @pl.when(ctx < distance)
        def _(place=place):
            far_t[:, place] = jnp.zeros((width, rows), BF16)
            ds_far[place, :] = jnp.zeros((rows, heads * rows), BF16)

    def query_grads(i, _):
        at = lanes(i * wide, wide)
        dq = dq_t[:, at] + dot_nn(far_t[...], ds_far[:, at])
        for j in range(wide):
            dq_ref[:, cols(i * wide + j)] = (
                dq[:, j * rows : (j + 1) * rows].T * F32(scale)
            ).astype(BF16)
        return 0

    lax.fori_loop(0, heads // wide, query_grads, 0)

    dk = acc_k[0] * F32(scale)
    dv = acc_v[0]
    for distance in (1, 2):

        @pl.when(reach >= distance)
        def _(distance=distance):
            for what in (0, 1):
                back_copy(distance, what).wait_recv()

        @pl.when(reach < distance)
        def _(distance=distance):
            for what in (0, 1):
                at = (distance - 1) * 2 + what
                back[at] = jnp.zeros_like(back[at])

        dk = dk + back[distance * 2 - 2].astype(F32)
        dv = dv + back[distance * 2 - 1].astype(F32)
    dk_ref[...] = dk.astype(BF16)
    dv_ref[...] = dv.astype(BF16)

    def end_g(h, _):
        g_copy(h).wait_send()
        return 0

    lax.fori_loop(0, heads, end_g, 0)
    for distance in (1, 2):

        @pl.when(reach >= distance)
        def _(distance=distance):
            for what in (0, 1, 2):
                window_copy(distance, what).wait_send()

        @pl.when(ctx >= distance)
        def _(distance=distance):
            for what in (0, 1):
                back_copy(distance, what).wait_send()


def put_out(dq_ref, dk_ref, dv_ref, dq_out, dk_out, dv_out, sem):
    copies = [
        pltpu.make_async_copy(dq_ref, dq_out.at[0], sem.at[0]),
        pltpu.make_async_copy(dk_ref, dk_out.at[0], sem.at[1]),
        pltpu.make_async_copy(dv_ref, dv_out.at[0], sem.at[2]),
    ]
    for copy in copies:
        copy.start()
    for copy in copies:
        copy.wait()


def per_device(n_section, n_ctx, queries, keys, values, attn_out, log_sums, grad_held, doc_ids):
    rows, width = keys.shape[1:]
    heads = log_sums.shape[1]
    hbm_spec = pl.BlockSpec(memory_space=pltpu.HBM)
    vmem_spec = pl.BlockSpec(memory_space=pltpu.VMEM)
    dq, dk, dv = pl.pallas_call(
        functools.partial(kernel, n_section, n_ctx, float(width) ** -0.5, WIDE),
        out_shape=(
            jax.ShapeDtypeStruct((rows, heads * width), BF16),
            jax.ShapeDtypeStruct((rows, width), BF16),
            jax.ShapeDtypeStruct((rows, width), BF16),
        ),
        in_specs=[hbm_spec] * 7,
        out_specs=(vmem_spec,) * 3,
        scratch_shapes=[
            pltpu.VMEM((heads, rows, width), BF16),
            pltpu.VMEM((heads, rows, width), BF16),
            pltpu.VMEM((heads, rows, width), BF16),
            pltpu.VMEM((3, rows, width), BF16),
            pltpu.VMEM((3, rows, width), BF16),
            pltpu.VMEM((3, 1, rows), jnp.int32),
            pltpu.VMEM((heads, rows), F32),
            pltpu.VMEM((1, heads * rows), F32),
            pltpu.VMEM((1, heads * rows), F32),
            pltpu.VMEM((1, heads * rows), F32),
            pltpu.VMEM((rows, rows), F32),
            pltpu.VMEM((heads, rows, rows), F32),
            pltpu.VMEM((width, heads * rows), F32),
            pltpu.VMEM((rows, heads * rows), F32),
            pltpu.VMEM((2 * rows, heads * rows), BF16),
            pltpu.VMEM((width, 2 * rows), BF16),
            pltpu.VMEM((3, rows, width), F32),
            pltpu.VMEM((3, rows, width), F32),
            pltpu.VMEM((4, rows, width), BF16),
            pltpu.VMEM((4, rows, width), BF16),
            pltpu.SemaphoreType.DMA((4 + 2 * heads,)),
            pltpu.SemaphoreType.DMA((heads,)),
            pltpu.SemaphoreType.DMA((heads,)),
            pltpu.SemaphoreType.DMA((6,)),
            pltpu.SemaphoreType.DMA((6,)),
            pltpu.SemaphoreType.DMA((4,)),
            pltpu.SemaphoreType.DMA((4,)),
            pltpu.SemaphoreType.REGULAR,
        ],
        compiler_params=pltpu.CompilerParams(
            collective_id=0, has_side_effects=True, vmem_limit_bytes=32 << 20
        ),
    )(
        *(
            pltpu.with_memory_space_constraint(operand, pltpu.HBM)
            for operand in (
                queries[0], keys[0], values[0], attn_out[0], log_sums[0], grad_held[0], doc_ids[None]
            )
        )
    )
    return pl.pallas_call(
        put_out,
        out_shape=tuple(jax.ShapeDtypeStruct((1,) + x.shape, x.dtype) for x in (dq, dk, dv)),
        in_specs=[vmem_spec] * 3,
        out_specs=(hbm_spec,) * 3,
        scratch_shapes=[pltpu.SemaphoreType.DMA((3,))],
        compiler_params=pltpu.CompilerParams(vmem_limit_bytes=4 << 20),
    )(dq, dk, dv)


def solution(mesh):
    placed = (
        P("section", "ctx", None),
        P("section", "ctx", None),
        P("section", "ctx", None),
        P("section", "ctx", None),
        P("section", None, "ctx"),
        P("section", "ctx", None),
        P("ctx"),
    )
    return jax.shard_map(
        functools.partial(per_device, mesh.shape["section"], mesh.shape["ctx"]),
        mesh=mesh,
        in_specs=placed,
        out_specs=(P("section", "ctx", None),) * 3,
        check_vma=False,
    )
```

```python
import functools
import math

import jax
import jax.numpy as jnp
from jax import lax
from jax.experimental import pallas as pl
from jax.experimental.pallas import tpu as pltpu
from jax.sharding import PartitionSpec as P

MESH = pl.DeviceIdType.MESH
LOG2E = math.log2(math.e)
FAR = 1e30
WIDE = 8
RUN = 64
F32 = jnp.float32
BF16 = jnp.bfloat16


def dot_nt(a, b):
    return lax.dot_general(a, b, (((1,), (1,)), ((), ())), preferred_element_type=F32)


def dot_nn(a, b):
    return lax.dot_general(a, b, (((1,), (0,)), ((), ())), preferred_element_type=F32)


def kernel(
    n_section, n_ctx, scale, wide,
    q_hbm, k_hbm, v_hbm, a_hbm, lse_hbm, g_hbm, doc_hbm,
    dq_ref, dk_ref, dv_ref,
    q_s, a_s, g_s, kw, vw, docs, lse_s, lse_row, far_row, del_row, bias, p32, dq_t,
    p_far, ds_far, far_t, acc_k, acc_v, part, back,
    local_sem, g_send, g_recv, w_send, w_recv, b_send, b_recv, go_sem,
):
    heads, rows, width = q_s.shape
    half = rows // 2
    sec = lax.axis_index("section")
    ctx = lax.axis_index("ctx")
    sec_up = lax.rem(sec + 1, n_section)
    sec_down = lax.rem(sec + n_section - 1, n_section)
    sooner = 2 - lax.rem(ctx, 2)
    later = 3 - sooner

    barrier = pltpu.get_barrier_semaphore()
    at_end = ((lax.rem(ctx, RUN) >= RUN - 2) & (ctx < n_ctx - 2)).astype(jnp.int32)
    before_end = ((lax.rem(ctx + 2, RUN) >= RUN - 2) & (ctx < n_ctx - 4)).astype(jnp.int32)
    odd = lax.rem(ctx, 2)
    end_odd = at_end * odd
    end_even = at_end - end_odd
    greeted = ctx - 2 * at_end
    pl.semaphore_signal(barrier, inc=1, device_id=(sec_up, greeted), device_id_type=MESH)
    for distance in (1, 2):

        @pl.when((ctx >= distance) & ((distance == 2) | (end_odd == 0)))
        def _(distance=distance):
            pl.semaphore_signal(
                barrier, inc=1, device_id=(sec, ctx - distance), device_id_type=MESH
            )

    def cols(h):
        return pl.ds(pl.multiple_of(h * width, width), width)

    def lanes(h, many):
        return pl.ds(pl.multiple_of(h * rows, rows), many * rows)

    fixed = [
        pltpu.make_async_copy(doc_hbm, docs.at[0], local_sem.at[0]),
        pltpu.make_async_copy(lse_hbm, lse_s, local_sem.at[1]),
        pltpu.make_async_copy(k_hbm, kw.at[0], local_sem.at[2]),
        pltpu.make_async_copy(v_hbm, vw.at[0], local_sem.at[3]),
    ]
    for copy in fixed:
        copy.start()

    def q_copy(h):
        return pltpu.make_async_copy(q_hbm.at[:, cols(h)], q_s.at[h], local_sem.at[4 + h])

    def a_copy(h):
        return pltpu.make_async_copy(
            a_hbm.at[:, cols(h)], a_s.at[h], local_sem.at[4 + heads + h]
        )

    def start_local(h, _):
        q_copy(h).start()
        a_copy(h).start()
        return 0

    lax.fori_loop(0, heads, start_local, 0)

    def g_copy(h):
        return pltpu.make_async_remote_copy(
            src_ref=g_hbm.at[:, cols(h)], dst_ref=g_s.at[h],
            send_sem=g_send.at[h], recv_sem=g_recv.at[h],
            device_id=(sec_down, ctx), device_id_type=MESH,
        )

    def window_copy(distance, what):
        src = (k_hbm, doc_hbm, v_hbm)[what]
        dst = (kw, docs, vw)[what].at[distance]
        at = (distance - 1) * 3 + what
        return pltpu.make_async_remote_copy(
            src_ref=src, dst_ref=dst,
            send_sem=w_send.at[at], recv_sem=w_recv.at[at],
            device_id=(sec, lax.rem(ctx + distance, n_ctx)), device_id_type=MESH,
        )

    def back_copy(distance, what):
        at = (distance - 1) * 2 + what
        return pltpu.make_async_remote_copy(
            src_ref=part.at[at], dst_ref=back.at[at],
            send_sem=b_send.at[at], recv_sem=b_recv.at[at],
            device_id=(sec, lax.rem(ctx + n_ctx - distance, n_ctx)), device_id_type=MESH,
        )

    reach = jnp.minimum(n_ctx - 1 - ctx, 2)
    pl.semaphore_wait(barrier, 1 + reach - at_end - end_even + before_end)

    @pl.when(before_end == 1)
    def _():
        pl.semaphore_signal(
            go_sem, inc=1, device_id=(sec, lax.rem(ctx + 2, n_ctx)), device_id_type=MESH
        )

    @pl.when(before_end * odd == 1)
    def _():
        pl.semaphore_signal(
            go_sem, inc=1, device_id=(sec, lax.rem(ctx + 1, n_ctx)), device_id_type=MESH
        )

    for distance in (sooner, later):

        @pl.when(reach >= distance)
        def _(distance=distance):
            for what in (0, 1, 2):
                window_copy(distance, what).start()

        if distance is sooner:

            @pl.when(end_even == 1)
            def _():
                pl.semaphore_wait(go_sem, 2)

    @pl.when(end_odd == 1)
    def _():
        pl.semaphore_wait(go_sem, 1)

    def start_g(h, _):
        g_copy(h).start()
        return 0

    lax.fori_loop(0, heads, start_g, 0)

    for copy in fixed:
        copy.wait()
    doc_row = docs[0].astype(F32)
    doc_col = jnp.broadcast_to(doc_row, (half, rows)).T
    doc_col = jnp.concatenate([doc_col, doc_col], axis=1)
    key_at = lax.broadcasted_iota(jnp.int32, (rows, rows), 0)
    query_at = lax.broadcasted_iota(jnp.int32, (rows, rows), 1)
    allowed = (doc_col == jnp.broadcast_to(doc_row, (rows, rows))) & (key_at <= query_at)
    bias[...] = jnp.where(allowed, F32(0.0), F32(-FAR))
    first = docs[0, :, 0:1]
    outside = jnp.where(docs[0] == first, F32(0.0), F32(FAR))
    c = F32(scale * LOG2E)
    for h in range(heads):
        row = lse_s[h : h + 1, :] * F32(LOG2E)
        lse_row[:, h * rows : (h + 1) * rows] = row
        far_row[:, h * rows : (h + 1) * rows] = row + outside

    def own_weights(h, _):
        q_copy(h).wait()
        lse = lse_row[:, lanes(h, 1)]
        s = dot_nt(kw[0, 0:half, :], q_s[h])
        p32[h, 0:half, :] = jnp.exp2(s * c - lse + bias[0:half, :])
        s = dot_nt(kw[0, half:rows, :], q_s[h, half:rows, :])
        p32[h, half:rows, half:rows] = jnp.exp2(s * c - lse[:, half:] + bias[half:, half:])
        return 0

    lax.fori_loop(0, heads, own_weights, 0)

    def turned(block):
        return block.astype(F32).T.astype(BF16)

    acc_k[...] = jnp.zeros_like(acc_k)
    acc_v[...] = jnp.zeros_like(acc_v)
    own_t = turned(kw[0])
    ones = jnp.ones((8, width), BF16)
    zeros = jnp.zeros((half, half), BF16)

    def own_grads(h, _):
        a_copy(h).wait()
        g_copy(h).wait_recv()
        g = g_s[h]
        product = g.astype(F32) * a_s[h].astype(F32)
        high = product.astype(BF16)
        low = (product - high.astype(F32)).astype(BF16)
        delta = (dot_nt(ones, high) + dot_nt(ones, low))[0:1, :]
        del_row[:, lanes(h, 1)] = delta
        p_top = p32[h, 0:half, :]
        p_low = p32[h, half:rows, half:rows]
        ds_top = (p_top * (dot_nt(vw[0, 0:half, :], g) - delta)).astype(BF16)
        ds_low = (
            p_low * (dot_nt(vw[0, half:rows, :], g[half:rows, :]) - delta[:, half:])
        ).astype(BF16)
        p = jnp.concatenate(
            [p_top.astype(BF16), jnp.concatenate([zeros, p_low.astype(BF16)], axis=1)], axis=0
        )
        ds = jnp.concatenate([ds_top, jnp.concatenate([zeros, ds_low], axis=1)], axis=0)
        acc_v[0] += dot_nn(p, g)
        acc_k[0] += dot_nn(ds, q_s[h])
        dq_t[:, lanes(h, 1)] = dot_nn(own_t, ds)
        return 0

    lax.fori_loop(0, heads, own_grads, 0)

    def heads_of(ref, i):
        return ref[pl.ds(i * wide, wide)].reshape(wide * rows, width)

    def far_block(distance, place):
        window_copy(distance, 0).wait_recv()
        window_copy(distance, 1).wait_recv()
        count = jnp.sum(
            jnp.where(docs[distance] == first, F32(1.0), F32(0.0)), axis=1, keepdims=True
        )

        def inside():
            at = lax.broadcasted_iota(jnp.int32, (rows, width), 0).astype(F32)
            return at >= jnp.broadcast_to(F32(rows) - count, (rows, width))

        def send(what, total):
            part[(distance - 1) * 2 + what] = jnp.where(inside(), total, 0.0).astype(BF16)
            back_copy(distance, what).start()

        k_in = jnp.where(inside(), kw[distance].astype(F32), 0.0)
        kw[distance] = k_in.astype(BF16)
        far_t[:, place] = k_in.T.astype(BF16)

        def weights(i, _):
            at = lanes(i * wide, wide)
            p = jnp.exp2(dot_nt(kw[distance], heads_of(q_s, i)) * c - far_row[:, at])
            p_far[:, at] = p
            acc_v[distance] += dot_nn(p.astype(BF16), heads_of(g_s, i))
            return 0

        lax.fori_loop(0, heads // wide, weights, 0)
        send(1, acc_v[distance])
        window_copy(distance, 2).wait_recv()
        vw[distance] = jnp.where(inside(), vw[distance].astype(F32), 0.0).astype(BF16)

        def score_grads(i, _):
            at = lanes(i * wide, wide)
            dp = dot_nt(vw[distance], heads_of(g_s, i))
            ds = (p_far[:, at] * (dp - del_row[:, at])).astype(BF16)
            ds_far[place, at] = ds
            acc_k[distance] += dot_nn(ds, heads_of(q_s, i))
            return 0

        lax.fori_loop(0, heads // wide, score_grads, 0)
        send(0, acc_k[distance] * F32(scale))

    for at, distance in enumerate((sooner, later)):
        place = slice(at * rows, (at + 1) * rows)

        @pl.when(ctx >= distance)
        def _(distance=distance, place=place):
            far_block(distance, place)

        @pl.when(ctx < distance)
        def _(place=place):
            far_t[:, place] = jnp.zeros((width, rows), BF16)
            ds_far[place, :] = jnp.zeros((rows, heads * rows), BF16)

    def query_grads(i, _):
        at = lanes(i * wide, wide)
        dq = dq_t[:, at] + dot_nn(far_t[...], ds_far[:, at])
        for j in range(wide):
            dq_ref[:, cols(i * wide + j)] = (
                dq[:, j * rows : (j + 1) * rows].T * F32(scale)
            ).astype(BF16)
        return 0

    lax.fori_loop(0, heads // wide, query_grads, 0)

    dk = acc_k[0] * F32(scale)
    dv = acc_v[0]
    for distance in (1, 2):

        @pl.when(reach >= distance)
        def _(distance=distance):
            for what in (0, 1):
                back_copy(distance, what).wait_recv()

        @pl.when(reach < distance)
        def _(distance=distance):
            for what in (0, 1):
                at = (distance - 1) * 2 + what
                back[at] = jnp.zeros_like(back[at])

        dk = dk + back[distance * 2 - 2].astype(F32)
        dv = dv + back[distance * 2 - 1].astype(F32)
    dk_ref[...] = dk.astype(BF16)
    dv_ref[...] = dv.astype(BF16)

    def end_g(h, _):
        g_copy(h).wait_send()
        return 0

    lax.fori_loop(0, heads, end_g, 0)
    for distance in (1, 2):

        @pl.when(reach >= distance)
        def _(distance=distance):
            for what in (0, 1, 2):
                window_copy(distance, what).wait_send()

        @pl.when(ctx >= distance)
        def _(distance=distance):
            for what in (0, 1):
                back_copy(distance, what).wait_send()


def put_out(dq_ref, dk_ref, dv_ref, dq_out, dk_out, dv_out, sem):
    copies = [
        pltpu.make_async_copy(dq_ref, dq_out.at[0], sem.at[0]),
        pltpu.make_async_copy(dk_ref, dk_out.at[0], sem.at[1]),
        pltpu.make_async_copy(dv_ref, dv_out.at[0], sem.at[2]),
    ]
    for copy in copies:
        copy.start()
    for copy in copies:
        copy.wait()


def per_device(n_section, n_ctx, queries, keys, values, attn_out, log_sums, grad_held, doc_ids):
    rows, width = keys.shape[1:]
    heads = log_sums.shape[1]
    hbm_spec = pl.BlockSpec(memory_space=pltpu.HBM)
    vmem_spec = pl.BlockSpec(memory_space=pltpu.VMEM)
    dq, dk, dv = pl.pallas_call(
        functools.partial(kernel, n_section, n_ctx, float(width) ** -0.5, WIDE),
        out_shape=(
            jax.ShapeDtypeStruct((rows, heads * width), BF16),
            jax.ShapeDtypeStruct((rows, width), BF16),
            jax.ShapeDtypeStruct((rows, width), BF16),
        ),
        in_specs=[hbm_spec] * 7,
        out_specs=(vmem_spec,) * 3,
        scratch_shapes=[
            pltpu.VMEM((heads, rows, width), BF16),
            pltpu.VMEM((heads, rows, width), BF16),
            pltpu.VMEM((heads, rows, width), BF16),
            pltpu.VMEM((3, rows, width), BF16),
            pltpu.VMEM((3, rows, width), BF16),
            pltpu.VMEM((3, 1, rows), jnp.int32),
            pltpu.VMEM((heads, rows), F32),
            pltpu.VMEM((1, heads * rows), F32),
            pltpu.VMEM((1, heads * rows), F32),
            pltpu.VMEM((1, heads * rows), F32),
            pltpu.VMEM((rows, rows), F32),
            pltpu.VMEM((heads, rows, rows), F32),
            pltpu.VMEM((width, heads * rows), F32),
            pltpu.VMEM((rows, heads * rows), F32),
            pltpu.VMEM((2 * rows, heads * rows), BF16),
            pltpu.VMEM((width, 2 * rows), BF16),
            pltpu.VMEM((3, rows, width), F32),
            pltpu.VMEM((3, rows, width), F32),
            pltpu.VMEM((4, rows, width), BF16),
            pltpu.VMEM((4, rows, width), BF16),
            pltpu.SemaphoreType.DMA((4 + 2 * heads,)),
            pltpu.SemaphoreType.DMA((heads,)),
            pltpu.SemaphoreType.DMA((heads,)),
            pltpu.SemaphoreType.DMA((6,)),
            pltpu.SemaphoreType.DMA((6,)),
            pltpu.SemaphoreType.DMA((4,)),
            pltpu.SemaphoreType.DMA((4,)),
            pltpu.SemaphoreType.REGULAR,
        ],
        compiler_params=pltpu.CompilerParams(
            collective_id=0, has_side_effects=True, vmem_limit_bytes=32 << 20
        ),
    )(
        *(
            pltpu.with_memory_space_constraint(operand, pltpu.HBM)
            for operand in (
                queries[0], keys[0], values[0], attn_out[0], log_sums[0], grad_held[0], doc_ids[None]
            )
        )
    )
    return pl.pallas_call(
        put_out,
        out_shape=tuple(jax.ShapeDtypeStruct((1,) + x.shape, x.dtype) for x in (dq, dk, dv)),
        in_specs=[vmem_spec] * 3,
        out_specs=(hbm_spec,) * 3,
        scratch_shapes=[pltpu.SemaphoreType.DMA((3,))],
        compiler_params=pltpu.CompilerParams(vmem_limit_bytes=4 << 20),
    )(dq, dk, dv)


def solution(mesh):
    placed = (
        P("section", "ctx", None),
        P("section", "ctx", None),
        P("section", "ctx", None),
        P("section", "ctx", None),
        P("section", None, "ctx"),
        P("section", "ctx", None),
        P("ctx"),
    )
    return jax.shard_map(
        functools.partial(per_device, mesh.shape["section"], mesh.shape["ctx"]),
        mesh=mesh,
        in_specs=placed,
        out_specs=(P("section", "ctx", None),) * 3,
        check_vma=False,
    )
```
